32 devices in a mesh: groups: 2 (over y), tile: 4 (over z), chan: 2 (over x), tm: 2 (over core).
Axes of the slice: x: 2, y: 2, z: 4, core: 2. Of those that a mesh axis runs over, the one named last changes fastest.
Arguments:
- latents: bfloat16 [8, 32, 576], P('tm', 'groups', 'tile'), parts along dimension 1, may hold values from -6 to 6
- tile_order: int32 [8], P('groups'), parts along dimension 0, may hold values from 0 to 3, each once
- w_in: bfloat16 [27, 16, 512], P(None, None, 'chan'), may hold values from -0.3125 to 0.3125
- gain_in: float32 [512], P('chan'), may hold values from 0.25 to 1.75
- shift_in: float32 [512], P('chan'), may hold values from -3 to 3
- w_mid: bfloat16 [27, 512, 512], P(None, None, 'chan'), may hold values from -0.0546875 to 0.0546875
- gain_mid: float32 [512], P('chan'), may hold values from 0.25 to 1.75
- shift_mid: float32 [512], P('chan'), may hold values from -3 to 3
- w_out: bfloat16 [3, 512], P(None, 'chan'), may hold values from -0.25 to 0.25
- blend_weight: float32 [8, 256], P('groups'), parts along dimension 0, may hold values from 0.25 to 4
Outputs:
- decoded: float32 [8, 6, 576], P('tm', 'groups', 'tile'), parts along dimension 1
The draws below stay inside these ranges and needn't reach their ends.
There are 2 independent parts, one for each index of `groups`. The reference program is written for one: setup_inputs(seed, part) draws one part's arguments, and reference() takes and returns one part's arrays. A program takes and returns all parts, laid end to end along the dimension named above; an argument that names none is the same for every part. Nothing has to cross between parts.
Inputs may be any that keep to these rules, and one draw needn't show every extreme that they name: `tile_order`: each image block is held by exactly one latent block.
All inputs are finite; a program needn't handle non-finite values.
Results may differ from the reference program's by a relative error of at most 0.0037.
Values may be sent and summed in bfloat16 or wider, within the bound.
A program may use at most 64 MiB of HBM per device.

```python
import math
import jax
import jax.numpy as jnp
from jax import lax

CH = 512
LATENT_CH = 16
GROUPS = 32
TSIDE = 16
STRIDE = 12
GRID_X = 4
FRAMES = 8
TILES = 4
PIXELS = 256
NPIX = 576


def level_of(own_key, shape, shards, least, high):
    factor_of = 1.0
    for dim, blocks in shards:
        draws = jax.random.uniform(jax.random.fold_in(jax.random.fold_in(own_key, 6), dim), (blocks,), jnp.float32, least / len(shards), high / len(shards))
        factor_of = factor_of * jnp.repeat(jnp.exp(draws), shape[dim] // blocks).reshape((-1,) + (1,) * (len(shape) - 1 - dim))
    return factor_of


def scatter_about(key, extent, scale, bound, pieces=(), kind=jnp.bfloat16):
    level = level_of(key, extent, pieces, -0.22, 0.18) if pieces else 1.0
    values = jax.random.normal(key, extent, jnp.float32) * scale * level
    return jnp.minimum(jnp.maximum(values, -bound), bound).astype(kind)


def setup_inputs(seed: int = 0, part: int = 0) -> dict:
    streams_of = jax.random.split(jax.random.key(seed), 11)
    own_keys = jax.random.split(jax.random.fold_in(streams_of[10], part), 11)
    latents = scatter_about(own_keys[0], (FRAMES, LATENT_CH, NPIX), 1.0, 6.0, ((0, 2), (2, 4)))
    tile_order = jax.random.permutation(own_keys[1], TILES).astype(jnp.int32)
    w_in = scatter_about(streams_of[2], (27, LATENT_CH, CH), (27 * LATENT_CH) ** -0.5, 0.3125, ((2, 2),))
    gain_in = jnp.clip(1.0 + 0.15 * jax.random.normal(streams_of[3], (CH,), jnp.float32), 0.25, 1.75)
    shift_in = scatter_about(streams_of[4], (CH,), 0.5, 3.0, ((0, 2),), jnp.float32)
    w_mid = scatter_about(streams_of[5], (27, CH, CH), (27 * CH) ** -0.5, 0.0546875, ((2, 2),))
    gain_mid = jnp.clip(1.0 + 0.15 * jax.random.normal(streams_of[6], (CH,), jnp.float32), 0.25, 1.75)
    shift_mid = scatter_about(streams_of[7], (CH,), 0.5, 3.0, ((0, 2),), jnp.float32)
    w_out = scatter_about(streams_of[8], (3, CH), CH ** -0.5, 0.25, ((1, 2),))
    blend_weight = jnp.clip(jnp.exp(jax.random.uniform(own_keys[9], (TILES, PIXELS), jnp.float32, math.log(0.25), math.log(4.0))), 0.25, 4.0)
    return {"latents": latents, "tile_order": tile_order, "w_in": w_in, "gain_in": gain_in, "shift_in": shift_in, "w_mid": w_mid, "gain_mid": gain_mid, "shift_mid": shift_mid, "w_out": w_out, "blend_weight": blend_weight}


EPSILON = 1e-06

def window_index(tile_id, tiles):
    slots = jnp.arange(TSIDE * TSIDE, dtype=jnp.int32)
    row = tile_id // GRID_X * STRIDE + slots // TSIDE
    col = tile_id % GRID_X * STRIDE + slots % TSIDE
    valid = (row < tiles // GRID_X * STRIDE) & (col < GRID_X * STRIDE)
    block = row // STRIDE * GRID_X + col // STRIDE
    index = block * (STRIDE * STRIDE) + row % STRIDE * STRIDE + col % STRIDE
    return (jnp.where(valid, index, 0).astype(jnp.int32), valid)

def causal_conv(values, weights, frames, side):
    pixels = side * side
    rows = jnp.arange(pixels, dtype=jnp.int32) // side
    cols = jnp.arange(pixels, dtype=jnp.int32) % side
    padded = jnp.concatenate([jnp.zeros((2,) + values.shape[1:], values.dtype), values], axis=0).astype(jnp.float32)
    weights = weights.astype(jnp.float32)
    total = jnp.zeros((frames, weights.shape[2], pixels), jnp.float32)
    for depth in range(3):
        window = padded[depth:depth + frames]
        for down in range(3):
            for across in range(3):
                offset = (down - 1) * side + (across - 1)
                inside = (rows + down - 1 >= 0) & (rows + down - 1 < side) & (cols + across - 1 >= 0) & (cols + across - 1 < side)
                moved = jnp.roll(window, -offset, axis=2)
                moved = jnp.where(inside[None, None, :], moved, jnp.zeros_like(moved))
                total = total + jnp.einsum('fcp,co->fop', moved, weights[9 * depth + 3 * down + across])
    return total

def normalize(values, gain, shift):
    frames, chans, pixels = values.shape
    width = CH // GROUPS
    grouped = values.reshape(frames, chans // width, width, pixels)
    count = frames * width * pixels
    mean = lax.optimization_barrier(jnp.sum(grouped, axis=(0, 2, 3))) / count
    variance = lax.optimization_barrier(jnp.sum(grouped * grouped, axis=(0, 2, 3))) / count - mean * mean
    scale = lax.rsqrt(variance + EPSILON)
    normed = (grouped - mean[None, :, None, None]) * scale[None, :, None, None]
    normed = normed.reshape(frames, chans, pixels) * gain[None, :, None] + shift[None, :, None]
    return jax.nn.silu(normed).astype(jnp.bfloat16)

def reference(latents, tile_order, w_in, gain_in, shift_in, w_mid, gain_mid, shift_mid, w_out, blend_weight):
    own = STRIDE * STRIDE
    blocks = latents.reshape(FRAMES, LATENT_CH, TILES, own)
    image = jnp.zeros_like(blocks).at[:, :, tile_order.astype(jnp.int32)].set(blocks)
    image = image.reshape(FRAMES, LATENT_CH, TILES * own)

    def accumulate(carry, tile_id):
        numer, denom = carry
        index, valid = window_index(tile_id, TILES)
        window = jnp.where(valid[None, None, :], jnp.take(image, index, axis=2), jnp.zeros((), jnp.bfloat16))
        first = causal_conv(window, w_in, FRAMES, TSIDE)
        hidden = normalize(first, gain_in, shift_in)
        second = causal_conv(hidden, w_mid, FRAMES, TSIDE)
        upper = normalize(second, gain_mid, shift_mid)
        color = jnp.einsum('oc,fcp->fop', w_out.astype(jnp.float32), upper.astype(jnp.float32))
        weight = jnp.where(valid, blend_weight[tile_id], jnp.float32(0.0))
        numer = numer.at[:, :, index].add(color * weight[None, None, :])
        denom = denom.at[index].add(weight)
        return ((numer, denom), None)
    start = (jnp.zeros((FRAMES, 3, TILES * own), jnp.float32), jnp.zeros((TILES * own,), jnp.float32))
    (numer, denom), _ = lax.scan(accumulate, start, jnp.arange(TILES, dtype=jnp.int32))
    return numer / denom[None, None, :]
```

```python
import functools

import jax
import jax.numpy as jnp
from jax import lax
from jax.experimental import pallas as pl
from jax.experimental.pallas import tpu as pltpu
from jax.sharding import PartitionSpec as P

GROUPS = 32
TSIDE = 16
STRIDE = 12
GRID_X = 4
EPSILON = 1e-06
LANES = 128
MESH = pl.DeviceIdType.MESH


def place_matrix(down, across, kind):
    pixels = TSIDE * TSIDE
    pixel = lax.broadcasted_iota(jnp.int32, (2 * LANES, pixels), 0)
    slot = lax.broadcasted_iota(jnp.int32, (2 * LANES, pixels), 1)
    row = slot // TSIDE - STRIDE * down
    col = slot % TSIDE - STRIDE * across
    inside = (row >= 0) & (row < STRIDE) & (col >= 0) & (col < STRIDE)
    hit = inside & (pixel == row * STRIDE + col)
    return jnp.where(hit, 1.0, 0.0).astype(kind)


def group_sums(sums, squares, width):
    chans = sums.shape[1]
    chunks = chans // LANES
    rows = [v[:, LANES * i : LANES * (i + 1)] for v in (sums, squares) for i in range(chunks)]
    if len(rows) < 8:
        rows.append(jnp.zeros((8 - len(rows), LANES), jnp.float32))
    stacked = jnp.concatenate(rows, axis=0)
    left = lax.broadcasted_iota(jnp.int32, (LANES, LANES), 0) // width
    right = lax.broadcasted_iota(jnp.int32, (LANES, LANES), 1) // width
    same = jnp.where(left == right, 1.0, 0.0).astype(jnp.float32)
    return jnp.dot(
        stacked, same, precision=lax.Precision.HIGHEST, preferred_element_type=jnp.float32
    )


def half_affine(stats, chans, count, gain, shift):
    chunks = chans // LANES
    sums = jnp.concatenate([stats[i : i + 1] for i in range(chunks)], axis=1)
    squares = jnp.concatenate([stats[chunks + i : chunks + i + 1] for i in range(chunks)], axis=1)
    mean = sums / count
    variance = squares / count - mean * mean
    scale = lax.rsqrt(variance + EPSILON) * gain
    return 0.5 * scale, 0.5 * (shift - mean * scale)


def silu_of_half(half):
    return half + half * jnp.tanh(half)


def kernel(
    sizes,
    lat_ref,
    order_ref,
    w_in_ref,
    gain_in_ref,
    shift_in_ref,
    w_mid_ref,
    gain_mid_ref,
    shift_mid_ref,
    w_out_ref,
    blend_ref,
    out_ref,
    lat,
    win,
    gains,
    shifts,
    mid,
    taps,
    first,
    hid,
    acc,
    place,
    stat_out,
    stat_in,
    col_out,
    col_in,
    local_sem,
    lat_s,
    lat_r,
    core_s,
    core_r,
    win_s,
    win_r,
    wcore_s,
    wcore_r,
    gain_s,
    gain_r,
    shift_s,
    shift_r,
    stat_s,
    stat_r,
    col_s,
    col_r,
):
    tiles, chan_count, cores = sizes
    frames, latent_ch, own = lat_ref.shape
    extra = own - LANES
    total_frames = frames * cores
    depth_taps, _, out_ch = w_in_ref.shape
    chans = out_ch * chan_count
    width = chans // GROUPS
    pixels = TSIDE * TSIDE
    tile_rows = tiles // GRID_X
    tile = lax.axis_index("tile")
    chan = lax.axis_index("chan")
    tm = lax.axis_index("tm")
    other = cores - 1 - tm
    split = depth_taps // 2
    parts = ((0, split), (split, depth_taps - split))

    def remote(src, dst, send, recv, device):
        return pltpu.make_async_remote_copy(
            src_ref=src,
            dst_ref=dst,
            send_sem=send,
            recv_sem=recv,
            device_id=device,
            device_id_type=MESH,
        )

    barrier = pltpu.get_barrier_semaphore()
    for far in range(tiles):
        for side in range(chan_count):
            if far or side:
                pl.semaphore_signal(
                    barrier,
                    inc=1,
                    device_id={
                        "tile": lax.rem(tile + far, tiles),
                        "chan": lax.rem(chan + side, chan_count),
                    },
                    device_id_type=MESH,
                )
    pl.semaphore_signal(barrier, inc=1, device_id={"tm": other}, device_id_type=MESH)

    own_win = pltpu.make_async_copy(w_in_ref, win.at[chan], local_sem.at[0])
    own_win.start()
    own_mid = pltpu.make_async_copy(w_mid_ref, mid, local_sem.at[1])
    own_mid.start()

    tail = jnp.zeros((latent_ch, LANES), jnp.float32)
    pixel = lax.broadcasted_iota(jnp.int32, (own, LANES), 0)
    lane = lax.broadcasted_iota(jnp.int32, (own, LANES), 1)
    for f in range(frames):
        lat[tm, tile, f] = lat_ref[f, :, 0:LANES]
        pick = (pixel >= LANES) & (lane == pixel - LANES + extra * f)
        tail = tail + jnp.dot(
            lat_ref[f],
            jnp.where(pick, 1.0, 0.0).astype(jnp.bfloat16),
            preferred_element_type=jnp.float32,
        )
    lat[tm, tile, frames] = tail.astype(jnp.bfloat16)
    blocks = [(down, across) for down in range(min(2, tile_rows)) for across in range(2)]
    for i, (down, across) in enumerate(blocks):
        place[i] = place_matrix(down, across, jnp.bfloat16)
    taps[0:2] = jnp.zeros((2,) + taps.shape[1:], taps.dtype)
    edge = jnp.zeros((TSIDE, hid.shape[2]), hid.dtype)
    for s in range(frames + 2):
        hid[s, 0:TSIDE] = edge
        hid[s, TSIDE + pixels : 2 * TSIDE + pixels] = edge
    col_out[...] = jnp.zeros_like(col_out)

    pl.semaphore_wait(barrier, tiles * chan_count)

    mine = lat.at[tm, tile]
    sends = []
    for t, (start, size) in enumerate(parts):

        @pl.when(tm == t)
        def _():
            for d in range(1, chan_count):
                remote(
                    w_in_ref.at[pl.ds(start, size)],
                    win.at[chan, pl.ds(start, size)],
                    win_s.at[d],
                    win_r.at[d],
                    {"chan": lax.rem(chan + d, chan_count)},
                ).start()

    for d in range(1, tiles):
        copy = remote(
            mine, mine, lat_s.at[d], lat_r.at[d], {"tile": lax.rem(tile + d, tiles)}
        )
        copy.start()
        sends.append(copy)
    copy = remote(mine, mine, core_s.at[0], core_r.at[0], {"tm": other})
    copy.start()
    sends.append(copy)
    for d in range(1, chan_count):
        to = {"chan": lax.rem(chan + d, chan_count)}
        for src, dst, send, recv in (
            (gain_in_ref, gains, gain_s, gain_r),
            (shift_in_ref, shifts, shift_s, shift_r),
        ):
            copy = remote(src, dst.at[chan], send.at[d], recv.at[d], to)
            copy.start()
            sends.append(copy)
    gains[chan] = gain_in_ref[...]
    shifts[chan] = shift_in_ref[...]

    for d in range(1, tiles):
        slot = lat.at[tm, lax.rem(tile - d + tiles, tiles)]
        remote(slot, slot, lat_s.at[d], lat_r.at[d], {"tm": other}).wait_recv()
        copy = remote(slot, slot, core_s.at[d], core_r.at[d], {"tm": other})
        copy.start()
        sends.append(copy)
    for t, (start, size) in enumerate(parts):

        @pl.when(tm == t)
        def _():
            for d in range(1, chan_count):
                slot = win.at[lax.rem(chan - d + chan_count, chan_count), pl.ds(start, size)]
                remote(slot, slot, win_s.at[d], win_r.at[d], {"tm": other}).wait_recv()
                remote(slot, slot, wcore_s.at[d], wcore_r.at[d], {"tm": other}).start()

    for d in range(tiles):
        slot = lat.at[other, lax.rem(tile - d + tiles, tiles)]
        remote(slot, slot, core_s.at[d], core_r.at[d], {"tm": other}).wait_recv()

    window = jnp.zeros((total_frames * latent_ch, pixels), jnp.float32)
    for i, (down, across) in enumerate(blocks):
        block = tile + GRID_X * down + across
        held = jnp.int32(0)
        for d in range(tiles):
            held = jnp.where(order_ref[d] == block, d, held)
        valid = (lax.rem(tile, GRID_X) + across < GRID_X) & (tile // GRID_X + down < tile_rows)
        rows = []
        for t in range(cores):
            message = lat[t, held].astype(jnp.float32)
            for f in range(frames):
                rest = message[frames]
                if f:
                    rest = pltpu.roll(rest, LANES - extra * f, 1)
                rows.append(jnp.concatenate([message[f], rest], axis=1))
        image = jnp.where(valid, jnp.concatenate(rows, axis=0), 0.0).astype(jnp.bfloat16)
        window = window + jnp.dot(image, place[i], preferred_element_type=jnp.float32)
    slot_id = lax.broadcasted_iota(jnp.int32, window.shape, 1)
    row, col = slot_id // TSIDE, slot_id % TSIDE
    for down in range(3):
        for across in range(3):
            offset = (down - 1) * TSIDE + across - 1
            moved = window if offset == 0 else pltpu.roll(window, -offset % pixels, 1)
            inside = (
                (row + down >= 1)
                & (row + down <= TSIDE)
                & (col + across >= 1)
                & (col + across <= TSIDE)
            )
            moved = jnp.where(inside, moved, 0.0).astype(jnp.bfloat16)
            at = (3 * down + across) * latent_ch
            taps[2 : 2 + total_frames, at : at + latent_ch, :] = moved.reshape(
                total_frames, latent_ch, pixels
            )

    own_win.wait()
    for t, (start, size) in enumerate(parts):

        @pl.when(tm != t)
        def _():
            for d in range(1, chan_count):
                slot = win.at[lax.rem(chan - d + chan_count, chan_count), pl.ds(start, size)]
                remote(slot, slot, wcore_s.at[d], wcore_r.at[d], {"tm": other}).wait_recv()

    def first_step(f, carry):
        patch = taps[pl.ds(f, 3)].reshape(depth_taps * latent_ch, pixels)
        sums, squares = [], []
        for c in range(chan_count):
            value = lax.dot_general(
                patch,
                win[c].reshape(depth_taps * latent_ch, out_ch),
                (((0,), (0,)), ((), ())),
                preferred_element_type=jnp.float32,
            )
            first[f, :, out_ch * c : out_ch * (c + 1)] = value
            folded = value.reshape(pixels // 8, 8, out_ch)
            sums.append(jnp.sum(folded, axis=0))
            squares.append(jnp.sum(folded * folded, axis=0))
        return (
            carry[0] + jnp.concatenate(sums, axis=1),
            carry[1] + jnp.concatenate(squares, axis=1),
        )

    zero = jnp.zeros((8, chans), jnp.float32)
    sums, squares = lax.fori_loop(0, total_frames, first_step, (zero, zero))
    for d in range(1, chan_count):
        slot_chan = lax.rem(chan - d + chan_count, chan_count)
        for dst, send, recv in ((gains, gain_s, gain_r), (shifts, shift_s, shift_r)):
            slot = dst.at[slot_chan]
            remote(slot, slot, send.at[d], recv.at[d], {"tm": other}).wait_recv()
    count = total_frames * width * pixels
    stats = group_sums(
        jnp.sum(sums, axis=0, keepdims=True), jnp.sum(squares, axis=0, keepdims=True), width
    )
    scale, offset = half_affine(
        stats,
        chans,
        count,
        jnp.concatenate([gains[c] for c in range(chan_count)], axis=1),
        jnp.concatenate([shifts[c] for c in range(chan_count)], axis=1),
    )

    step_rows = 2 * TSIDE
    col = lax.broadcasted_iota(jnp.int32, (step_rows, chans), 0) % TSIDE

    def hidden_step(s, _):
        frame = frames * tm - 2 + s
        known = frame >= 0
        frame = jnp.maximum(frame, 0)
        for r in range(pixels // step_rows):
            value = silu_of_half(
                first[frame, step_rows * r : step_rows * (r + 1), :] * scale + offset
            )
            value = jnp.where(known, value, 0.0)
            before = jnp.where(col == 0, 0.0, pltpu.roll(value, 1, 0))
            after = jnp.where(col == TSIDE - 1, 0.0, pltpu.roll(value, step_rows - 1, 0))
            for e, piece in enumerate((before, value, after)):
                hid[
                    s,
                    TSIDE + step_rows * r : TSIDE + step_rows * (r + 1),
                    chans * e : chans * (e + 1),
                ] = piece.astype(jnp.bfloat16)
        return 0

    lax.fori_loop(0, frames + 2, hidden_step, 0)
    own_mid.wait()

    batch = 2 if frames % 2 == 0 else 1

    def second_step(g, carry):
        total = None
        for a in range(3):
            for b in range(3):
                value = jnp.dot(
                    hid[pl.ds(batch * g + a, batch), TSIDE * b : TSIDE * b + pixels, :].reshape(
                        batch * pixels, 3 * chans
                    ),
                    mid[9 * a + 3 * b : 9 * a + 3 * b + 3].reshape(3 * chans, out_ch),
                    preferred_element_type=jnp.float32,
                )
                total = value if total is None else total + value
        acc[pl.ds(batch * g, batch)] = total.reshape(batch, pixels, out_ch)
        folded = total.reshape(batch * pixels // 8, 8, out_ch)
        return (
            carry[0] + jnp.sum(folded, axis=0),
            carry[1] + jnp.sum(folded * folded, axis=0),
        )

    zero = jnp.zeros((8, out_ch), jnp.float32)
    sums, squares = lax.fori_loop(0, frames // batch, second_step, (zero, zero))
    stats = group_sums(
        jnp.sum(sums, axis=0, keepdims=True), jnp.sum(squares, axis=0, keepdims=True), width
    )
    stat_out[...] = stats
    stat_copy = remote(stat_out, stat_in, stat_s, stat_r, {"tm": other})
    stat_copy.start()
    stat_copy.wait()
    stats = stats + stat_in[...]
    scale, offset = half_affine(stats, out_ch, count, gain_mid_ref[...], shift_mid_ref[...])
    colors = out_ref.shape[1]
    for f in range(frames):
        upper = silu_of_half(acc[f] * scale + offset).astype(jnp.bfloat16)
        col_out[colors * f : colors * (f + 1), :] = lax.dot_general(
            w_out_ref[...], upper, (((1,), (1,)), ((), ())), preferred_element_type=jnp.float32
        )

    def tile_valid_to(down, across):
        return (lax.rem(tile, GRID_X) + across < GRID_X) & (tile // GRID_X + down < tile_rows)

    def tile_valid_from(down, across):
        return (lax.rem(tile, GRID_X) >= across) & (tile // GRID_X >= down)

    def color_copy(i, d, hop):
        return remote(
            col_out,
            col_in.at[i, d],
            col_s.at[i, d],
            col_r.at[i, d],
            {
                "tile": lax.rem(tile + hop, tiles),
                "chan": lax.rem(chan + d, chan_count),
            },
        )

    for i, (down, across) in reversed(list(enumerate(blocks))):
        for d in reversed(range(chan_count)):
            if i or d:
                pl.when(tile_valid_to(down, across))(
                    color_copy(i, d, GRID_X * down + across).start
                )

    rows = col_out.shape[0]
    row_id = lax.broadcasted_iota(jnp.int32, (rows, pixels), 0)
    blended = jnp.zeros((rows, 2 * LANES), jnp.float32)
    for i, (down, across) in enumerate(blocks):
        hop = GRID_X * down + across
        here = tile_valid_from(down, across)
        for d in range(chan_count):
            if i or d:
                pl.when(here)(color_copy(i, d, hop).wait_recv)
        color = col_out[...] if i == 0 else col_in[i, 0]
        for d in range(1, chan_count):
            color = color + col_in[i, d]
        weight = blend_ref[pl.ds(lax.rem(tile - hop + tiles, tiles), 1), :]
        color = jnp.where(row_id == colors * frames, 1.0, color) * weight
        color = jnp.where(here, color, 0.0)
        blended = blended + lax.dot_general(
            color,
            place[i].astype(jnp.float32),
            (((1,), (1,)), ((), ())),
            precision=lax.Precision.HIGHEST,
            preferred_element_type=jnp.float32,
        )
    result = blended / blended[colors * frames : colors * frames + 1]
    for f in range(frames):
        out_ref[f] = result[colors * f : colors * (f + 1), :own]

    for copy in sends:
        copy.wait_send()
    for t, (start, size) in enumerate(parts):

        @pl.when(tm == t)
        def _():
            for d in range(1, chan_count):
                slot = win.at[lax.rem(chan - d + chan_count, chan_count), pl.ds(start, size)]
                remote(slot, slot, win_s.at[d], win_r.at[d], {"tm": other}).wait_send()
                remote(slot, slot, wcore_s.at[d], wcore_r.at[d], {"tm": other}).wait_send()

    for i, (down, across) in enumerate(blocks):
        for d in range(chan_count):
            if i or d:
                pl.when(tile_valid_to(down, across))(
                    color_copy(i, d, GRID_X * down + across).wait_send
                )


def body(
    sizes,
    latents,
    tile_order,
    w_in,
    gain_in,
    shift_in,
    w_mid,
    gain_mid,
    shift_mid,
    w_out,
    blend_weight,
):
    tiles, chan_count, cores = sizes
    frames, latent_ch, own = latents.shape
    depth_taps, chans, out_ch = w_mid.shape
    total_frames = frames * cores
    pixels = TSIDE * TSIDE
    colors = w_out.shape[0]
    vmem = pl.BlockSpec(memory_space=pltpu.VMEM)
    anywhere = pl.BlockSpec(memory_space=pl.ANY)
    bf16, f32 = jnp.bfloat16, jnp.float32
    block_count = 2 * min(2, tiles // GRID_X)
    color_rows = -(-(colors * frames + 1) // 8) * 8
    dma = pltpu.SemaphoreType.DMA
    scratch = [
        pltpu.VMEM((cores, tiles, frames + 1, latent_ch, LANES), bf16),
        pltpu.VMEM((chan_count, depth_taps, latent_ch, out_ch), bf16),
        pltpu.VMEM((chan_count, 1, out_ch), f32),
        pltpu.VMEM((chan_count, 1, out_ch), f32),
        pltpu.VMEM((depth_taps, chans, out_ch), bf16),
        pltpu.VMEM((total_frames + 2, 9 * latent_ch, pixels), bf16),
        pltpu.VMEM((total_frames, pixels, chans), f32),
        pltpu.VMEM((frames + 2, pixels + 2 * TSIDE, 3 * chans), bf16),
        pltpu.VMEM((frames, pixels, out_ch), f32),
        pltpu.VMEM((block_count, 2 * LANES, pixels), bf16),
        pltpu.VMEM((8, LANES), f32),
        pltpu.VMEM((8, LANES), f32),
        pltpu.VMEM((color_rows, pixels), f32),
        pltpu.VMEM((block_count, chan_count, color_rows, pixels), f32),
        dma((2,)),
        dma((tiles,)),
        dma((tiles,)),
        dma((tiles,)),
        dma((tiles,)),
    ]
    scratch += [dma((chan_count,)) for _ in range(8)]
    scratch += [dma, dma, dma((block_count, chan_count)), dma((block_count, chan_count))]
    return pl.pallas_call(
        functools.partial(kernel, sizes),
        out_shape=jax.ShapeDtypeStruct((frames, colors, own), f32),
        in_specs=[
            vmem,
            pl.BlockSpec(memory_space=pltpu.SMEM),
            anywhere,
            vmem,
            vmem,
            anywhere,
            vmem,
            vmem,
            vmem,
            vmem,
        ],
        out_specs=vmem,
        scratch_shapes=scratch,
        compiler_params=pltpu.CompilerParams(collective_id=0, has_side_effects=True),
    )(
        latents,
        tile_order,
        w_in,
        gain_in.reshape(1, -1),
        shift_in.reshape(1, -1),
        w_mid,
        gain_mid.reshape(1, -1),
        shift_mid.reshape(1, -1),
        w_out,
        blend_weight,
    )


def solution(mesh):
    placed = (
        P("tm", "groups", "tile"),
        P("groups"),
        P(None, None, "chan"),
        P("chan"),
        P("chan"),
        P(None, None, "chan"),
        P("chan"),
        P("chan"),
        P(None, "chan"),
        P("groups", None),
    )
    sizes = (mesh.shape["tile"], mesh.shape["chan"], mesh.shape["tm"])
    return jax.shard_map(
        functools.partial(body, sizes),
        mesh=mesh,
        in_specs=placed,
        out_specs=P("tm", "groups", "tile"),
        check_vma=False,
    )
```

```python
import functools

import jax
import jax.numpy as jnp
from jax import lax
from jax.experimental import pallas as pl
from jax.experimental.pallas import tpu as pltpu
from jax.sharding import PartitionSpec as P

GROUPS = 32
TSIDE = 16
STRIDE = 12
GRID_X = 4
EPSILON = 1e-06
LANES = 128
MESH = pl.DeviceIdType.MESH


def place_matrix(down, across, kind):
    pixels = TSIDE * TSIDE
    pixel = lax.broadcasted_iota(jnp.int32, (2 * LANES, pixels), 0)
    slot = lax.broadcasted_iota(jnp.int32, (2 * LANES, pixels), 1)
    row = slot // TSIDE - STRIDE * down
    col = slot % TSIDE - STRIDE * across
    inside = (row >= 0) & (row < STRIDE) & (col >= 0) & (col < STRIDE)
    hit = inside & (pixel == row * STRIDE + col)
    return jnp.where(hit, 1.0, 0.0).astype(kind)


def group_sums(sums, squares, width):
    chans = sums.shape[1]
    chunks = chans // LANES
    rows = [v[:, LANES * i : LANES * (i + 1)] for v in (sums, squares) for i in range(chunks)]
    if len(rows) < 8:
        rows.append(jnp.zeros((8 - len(rows), LANES), jnp.float32))
    stacked = jnp.concatenate(rows, axis=0)
    left = lax.broadcasted_iota(jnp.int32, (LANES, LANES), 0) // width
    right = lax.broadcasted_iota(jnp.int32, (LANES, LANES), 1) // width
    same = jnp.where(left == right, 1.0, 0.0).astype(jnp.float32)
    return jnp.dot(
        stacked, same, precision=lax.Precision.HIGHEST, preferred_element_type=jnp.float32
    )


def half_affine(stats, chans, count, gain, shift):
    chunks = chans // LANES
    sums = jnp.concatenate([stats[i : i + 1] for i in range(chunks)], axis=1)
    squares = jnp.concatenate([stats[chunks + i : chunks + i + 1] for i in range(chunks)], axis=1)
    mean = sums / count
    variance = squares / count - mean * mean
    scale = lax.rsqrt(variance + EPSILON) * gain
    return 0.5 * scale, 0.5 * (shift - mean * scale)


def silu_of_half(half):
    return half + half * jnp.tanh(half)


def kernel(
    sizes,
    lat_hbm,
    order_hbm,
    w_in_ref,
    gain_in_ref,
    shift_in_ref,
    w_mid_ref,
    gain_mid_hbm,
    shift_mid_hbm,
    w_out_hbm,
    blend_hbm,
    out_ref,
    lat_ref,
    order_ref,
    gain_mid_ref,
    shift_mid_ref,
    w_out_ref,
    blend_ref,
    first_sums,
    lat,
    win,
    gains,
    shifts,
    mid,
    taps,
    first,
    hid,
    acc,
    place,
    stat_out,
    stat_in,
    col_out,
    col_in,
    local_sem,
    lat_s,
    lat_r,
    core_s,
    core_r,
    win_s,
    win_r,
    wcore_s,
    wcore_r,
    gain_s,
    gain_r,
    shift_s,
    shift_r,
    stat_s,
    stat_r,
    col_s,
    col_r,
):
    tiles, chan_count, cores = sizes
    frames, latent_ch, own = lat_hbm.shape
    extra = own - LANES
    total_frames = frames * cores
    depth_taps, _, out_ch = w_in_ref.shape
    chans = out_ch * chan_count
    width = chans // GROUPS
    pixels = TSIDE * TSIDE
    tile_rows = tiles // GRID_X
    tile = lax.axis_index("tile")
    chan = lax.axis_index("chan")
    tm = lax.axis_index("tm")
    other = cores - 1 - tm
    split = depth_taps // 2
    parts = ((0, split), (split, depth_taps - split))

    def remote(src, dst, send, recv, device):
        return pltpu.make_async_remote_copy(
            src_ref=src,
            dst_ref=dst,
            send_sem=send,
            recv_sem=recv,
            device_id=device,
            device_id_type=MESH,
        )

    barrier = pltpu.get_barrier_semaphore()
    for far in range(tiles):
        for side in range(chan_count):
            if far or side:
                pl.semaphore_signal(
                    barrier,
                    inc=1,
                    device_id={
                        "tile": lax.rem(tile + far, tiles),
                        "chan": lax.rem(chan + side, chan_count),
                    },
                    device_id_type=MESH,
                )
    pl.semaphore_signal(barrier, inc=1, device_id={"tm": other}, device_id_type=MESH)

    pairs = (
        (lat_hbm, lat_ref),
        (order_hbm, order_ref),
        (w_in_ref, win.at[chan]),
        (gain_in_ref, gains.at[chan]),
        (shift_in_ref, shifts.at[chan]),
        (gain_mid_hbm, gain_mid_ref),
        (shift_mid_hbm, shift_mid_ref),
        (w_out_hbm, w_out_ref),
        (blend_hbm, blend_ref),
        (w_mid_ref, mid),
    )
    loads = [
        pltpu.make_async_copy(src, dst, local_sem.at[i]) for i, (src, dst) in enumerate(pairs)
    ]
    for load in loads:
        load.start()

    blocks = [(down, across) for down in range(min(2, tile_rows)) for across in range(2)]
    for i, (down, across) in enumerate(blocks):
        place[i] = place_matrix(down, across, jnp.bfloat16)

    tail = jnp.zeros((latent_ch, LANES), jnp.float32)
    pixel = lax.broadcasted_iota(jnp.int32, (own, LANES), 0)
    lane = lax.broadcasted_iota(jnp.int32, (own, LANES), 1)
    loads[0].wait()
    for f in range(frames):
        lat[tm, tile, f] = lat_ref[f, :, 0:LANES]
        pick = (pixel >= LANES) & (lane == pixel - LANES + extra * f)
        tail = tail + jnp.dot(
            lat_ref[f],
            jnp.where(pick, 1.0, 0.0).astype(jnp.bfloat16),
            preferred_element_type=jnp.float32,
        )
    lat[tm, tile, frames] = tail.astype(jnp.bfloat16)
    taps[0:2] = jnp.zeros((2,) + taps.shape[1:], taps.dtype)
    edge = jnp.zeros((TSIDE, hid.shape[2]), hid.dtype)
    for s in range(frames + 2):
        hid[s, 0:TSIDE] = edge
        hid[s, TSIDE + pixels : 2 * TSIDE + pixels] = edge
    col_out[...] = jnp.zeros_like(col_out)

    pl.semaphore_wait(barrier, tiles * chan_count)

    mine = lat.at[tm, tile]
    sends = []
    for t, (start, size) in enumerate(parts):

        @pl.when(tm == t)
        def _():
            for d in range(1, chan_count):
                remote(
                    w_in_ref.at[pl.ds(start, size)],
                    win.at[chan, pl.ds(start, size)],
                    win_s.at[d],
                    win_r.at[d],
                    {"chan": lax.rem(chan + d, chan_count)},
                ).start()

    for step in range(1, tiles):
        d = jnp.where(2 * tile < tiles, tiles - step, step)
        copy = remote(
            mine, mine, lat_s.at[d], lat_r.at[d], {"tile": lax.rem(tile + d, tiles)}
        )
        copy.start()
        sends.append(copy)
    copy = remote(mine, mine, core_s.at[0], core_r.at[0], {"tm": other})
    copy.start()
    sends.append(copy)
    for d in range(1, chan_count):
        to = {"chan": lax.rem(chan + d, chan_count)}
        for src, dst, send, recv in (
            (gain_in_ref, gains, gain_s, gain_r),
            (shift_in_ref, shifts, shift_s, shift_r),
        ):
            copy = remote(src, dst.at[chan], send.at[d], recv.at[d], to)
            copy.start()
            sends.append(copy)

    for d in range(1, tiles):
        slot = lat.at[tm, lax.rem(tile - d + tiles, tiles)]
        remote(slot, slot, lat_s.at[d], lat_r.at[d], {"tm": other}).wait_recv()
        copy = remote(slot, slot, core_s.at[d], core_r.at[d], {"tm": other})
        copy.start()
        sends.append(copy)
    for t, (start, size) in enumerate(parts):

        @pl.when(tm == t)
        def _():
            for d in range(1, chan_count):
                slot = win.at[lax.rem(chan - d + chan_count, chan_count), pl.ds(start, size)]
                remote(slot, slot, win_s.at[d], win_r.at[d], {"tm": other}).wait_recv()
                remote(slot, slot, wcore_s.at[d], wcore_r.at[d], {"tm": other}).start()

    for d in range(tiles):
        slot = lat.at[other, lax.rem(tile - d + tiles, tiles)]
        remote(slot, slot, core_s.at[d], core_r.at[d], {"tm": other}).wait_recv()

    loads[1].wait()
    window = jnp.zeros((total_frames * latent_ch, pixels), jnp.float32)
    for i, (down, across) in enumerate(blocks):
        block = tile + GRID_X * down + across
        held = jnp.int32(0)
        for d in range(tiles):
            held = jnp.where(order_ref[d] == block, d, held)
        valid = (lax.rem(tile, GRID_X) + across < GRID_X) & (tile // GRID_X + down < tile_rows)
        rows = []
        for t in range(cores):
            message = lat[t, held].astype(jnp.float32)
            for f in range(frames):
                rest = message[frames]
                if f:
                    rest = pltpu.roll(rest, LANES - extra * f, 1)
                rows.append(jnp.concatenate([message[f], rest], axis=1))
        image = jnp.where(valid, jnp.concatenate(rows, axis=0), 0.0).astype(jnp.bfloat16)
        window = window + jnp.dot(image, place[i], preferred_element_type=jnp.float32)
    slot_id = lax.broadcasted_iota(jnp.int32, window.shape, 1)
    row, col = slot_id // TSIDE, slot_id % TSIDE
    for down in range(3):
        for across in range(3):
            offset = (down - 1) * TSIDE + across - 1
            moved = window if offset == 0 else pltpu.roll(window, -offset % pixels, 1)
            inside = (
                (row + down >= 1)
                & (row + down <= TSIDE)
                & (col + across >= 1)
                & (col + across <= TSIDE)
            )
            moved = jnp.where(inside, moved, 0.0).astype(jnp.bfloat16)
            at = (3 * down + across) * latent_ch
            taps[2 : 2 + total_frames, at : at + latent_ch, :] = moved.reshape(
                total_frames, latent_ch, pixels
            )

    loads[2].wait()
    zero = jnp.zeros((8, out_ch), jnp.float32)
    for d in range(chan_count):
        source = lax.rem(chan - d + chan_count, chan_count)
        if d:
            for t, (start, size) in enumerate(parts):

                @pl.when(tm != t)
                def _():
                    slot = win.at[source, pl.ds(start, size)]
                    remote(slot, slot, wcore_s.at[d], wcore_r.at[d], {"tm": other}).wait_recv()

        def first_step(g, carry):
            sums, squares = carry
            for f in (2 * g, 2 * g + 1):
                value = lax.dot_general(
                    taps[pl.ds(f, 3)].reshape(depth_taps * latent_ch, pixels),
                    win[source].reshape(depth_taps * latent_ch, out_ch),
                    (((0,), (0,)), ((), ())),
                    preferred_element_type=jnp.float32,
                )
                first[source, f] = value
                folded = value.reshape(pixels // 8, 8, out_ch)
                sums = sums + jnp.sum(folded, axis=0)
                squares = squares + jnp.sum(folded * folded, axis=0)
            return sums, squares

        sums, squares = lax.fori_loop(0, total_frames // 2, first_step, (zero, zero))
        first_sums[source, 0:1] = jnp.sum(sums, axis=0, keepdims=True)
        first_sums[source, 1:2] = jnp.sum(squares, axis=0, keepdims=True)
    for load in loads[3:9]:
        load.wait()
    for d in range(1, chan_count):
        slot_chan = lax.rem(chan - d + chan_count, chan_count)
        for dst, send, recv in ((gains, gain_s, gain_r), (shifts, shift_s, shift_r)):
            slot = dst.at[slot_chan]
            remote(slot, slot, send.at[d], recv.at[d], {"tm": other}).wait_recv()
    count = total_frames * width * pixels
    stats = group_sums(
        jnp.concatenate([first_sums[c, 0:1] for c in range(chan_count)], axis=1),
        jnp.concatenate([first_sums[c, 1:2] for c in range(chan_count)], axis=1),
        width,
    )
    scale, offset = half_affine(
        stats,
        chans,
        count,
        jnp.concatenate([gains[c] for c in range(chan_count)], axis=1),
        jnp.concatenate([shifts[c] for c in range(chan_count)], axis=1),
    )

    step_rows = 2 * TSIDE
    steps = pixels // step_rows
    col = lax.broadcasted_iota(jnp.int32, (step_rows, out_ch), 0) % TSIDE

    def hidden_rows(s, r):
        frame = frames * tm - 2 + s
        known = frame >= 0
        frame = jnp.maximum(frame, 0)
        for c in range(chan_count):
            channels = slice(out_ch * c, out_ch * (c + 1))
            value = silu_of_half(
                first[c, frame, step_rows * r : step_rows * (r + 1), :] * scale[:, channels]
                + offset[:, channels]
            )
            value = jnp.where(known, value, 0.0)
            before = jnp.where(col == 0, 0.0, pltpu.roll(value, 1, 0))
            after = jnp.where(col == TSIDE - 1, 0.0, pltpu.roll(value, step_rows - 1, 0))
            for e, piece in enumerate((before, value, after)):
                hid[
                    s,
                    TSIDE + step_rows * r : TSIDE + step_rows * (r + 1),
                    chans * e + out_ch * c : chans * e + out_ch * (c + 1),
                ] = piece.astype(jnp.bfloat16)

    def hidden_step(s, carry):
        for r in range(steps):
            hidden_rows(s, r)
        return carry

    batch = 2 if frames % 2 == 0 else 1
    lax.fori_loop(0, batch + 2, hidden_step, 0)
    loads[9].wait()

    sums = squares = jnp.zeros((8, out_ch), jnp.float32)
    for at in range(0, frames, batch):
        ahead = [
            (s, r)
            for s in range(at + batch + 2, min(at + 2 * batch, frames) + 2)
            for r in range(steps)
        ]
        share = -(-len(ahead) // 9)
        total = None
        for a in range(3):
            for b in range(3):
                value = jnp.dot(
                    hid[at + a : at + a + batch, TSIDE * b : TSIDE * b + pixels, :].reshape(
                        batch * pixels, 3 * chans
                    ),
                    mid[9 * a + 3 * b : 9 * a + 3 * b + 3].reshape(3 * chans, out_ch),
                    preferred_element_type=jnp.float32,
                )
                total = value if total is None else total + value
                for s, r in ahead[share * (3 * a + b) : share * (3 * a + b + 1)]:
                    hidden_rows(s, r)
        acc[at : at + batch] = total.reshape(batch, pixels, out_ch)
        folded = total.reshape(batch * pixels // 8, 8, out_ch)
        sums = sums + jnp.sum(folded, axis=0)
        squares = squares + jnp.sum(folded * folded, axis=0)
    stats = group_sums(
        jnp.sum(sums, axis=0, keepdims=True), jnp.sum(squares, axis=0, keepdims=True), width
    )
    stat_out[...] = stats
    stat_copy = remote(stat_out, stat_in, stat_s, stat_r, {"tm": other})
    stat_copy.start()
    stat_copy.wait()
    stats = stats + stat_in[...]
    scale, offset = half_affine(stats, out_ch, count, gain_mid_ref[...], shift_mid_ref[...])
    colors = out_ref.shape[0]
    for f in range(frames):
        upper = silu_of_half(acc[f] * scale + offset).astype(jnp.bfloat16)
        color = lax.dot_general(
            w_out_ref[...], upper, (((1,), (1,)), ((), ())), preferred_element_type=jnp.float32
        )
        for o in range(colors):
            col_out[frames * o + f : frames * o + f + 1, :] = color[o : o + 1]

    def tile_valid_to(down, across):
        return (lax.rem(tile, GRID_X) + across < GRID_X) & (tile // GRID_X + down < tile_rows)

    def tile_valid_from(down, across):
        return (lax.rem(tile, GRID_X) >= across) & (tile // GRID_X >= down)

    def color_copy(i, d, hop):
        return remote(
            col_out,
            col_in.at[i, d],
            col_s.at[i, d],
            col_r.at[i, d],
            {
                "tile": lax.rem(tile + hop, tiles),
                "chan": lax.rem(chan + d, chan_count),
            },
        )

    for i, (down, across) in reversed(list(enumerate(blocks))):
        for d in reversed(range(chan_count)):
            if i or d:
                pl.when(tile_valid_to(down, across))(
                    color_copy(i, d, GRID_X * down + across).start
                )

    rows = col_out.shape[0]
    row_id = lax.broadcasted_iota(jnp.int32, (rows, pixels), 0)
    blended = jnp.zeros((rows, 2 * LANES), jnp.float32)
    for i, (down, across) in enumerate(blocks):
        hop = GRID_X * down + across
        here = tile_valid_from(down, across)
        for d in range(chan_count):
            if i or d:
                pl.when(here)(color_copy(i, d, hop).wait_recv)
        color = col_out[...] if i == 0 else col_in[i, 0]
        for d in range(1, chan_count):
            color = color + col_in[i, d]
        weight = blend_ref[pl.ds(lax.rem(tile - hop + tiles, tiles), 1), :]
        color = jnp.where(row_id == colors * frames, 1.0, color) * weight
        color = jnp.where(here, color, 0.0)
        blended = blended + lax.dot_general(
            color,
            place[i].astype(jnp.float32),
            (((1,), (1,)), ((), ())),
            precision=lax.Precision.HIGHEST,
            preferred_element_type=jnp.float32,
        )
    result = blended / blended[colors * frames : colors * frames + 1]
    for o in range(colors):
        out_ref[o] = result[frames * o : frames * (o + 1), :own]

    for copy in sends:
        copy.wait_send()
    for t, (start, size) in enumerate(parts):

        @pl.when(tm == t)
        def _():
            for d in range(1, chan_count):
                slot = win.at[lax.rem(chan - d + chan_count, chan_count), pl.ds(start, size)]
                remote(slot, slot, win_s.at[d], win_r.at[d], {"tm": other}).wait_send()
                remote(slot, slot, wcore_s.at[d], wcore_r.at[d], {"tm": other}).wait_send()

    for i, (down, across) in enumerate(blocks):
        for d in range(chan_count):
            if i or d:
                pl.when(tile_valid_to(down, across))(
                    color_copy(i, d, GRID_X * down + across).wait_send
                )


def body(
    sizes,
    latents,
    tile_order,
    w_in,
    gain_in,
    shift_in,
    w_mid,
    gain_mid,
    shift_mid,
    w_out,
    blend_weight,
):
    tiles, chan_count, cores = sizes
    frames, latent_ch, own = latents.shape
    depth_taps, chans, out_ch = w_mid.shape
    total_frames = frames * cores
    pixels = TSIDE * TSIDE
    colors = w_out.shape[0]
    vmem = pl.BlockSpec(memory_space=pltpu.VMEM)
    anywhere = pl.BlockSpec(memory_space=pl.ANY)
    bf16, f32 = jnp.bfloat16, jnp.float32
    block_count = 2 * min(2, tiles // GRID_X)
    color_rows = -(-(colors * frames + 1) // 8) * 8
    dma = pltpu.SemaphoreType.DMA
    smem = pltpu.SMEM
    scratch = [
        pltpu.VMEM(latents.shape, bf16),
        smem(tile_order.shape, jnp.int32),
        pltpu.VMEM((1, out_ch), f32),
        pltpu.VMEM((1, out_ch), f32),
        pltpu.VMEM(w_out.shape, bf16),
        pltpu.VMEM(blend_weight.shape, f32),
        pltpu.VMEM((chan_count, 8, out_ch), f32),
        pltpu.VMEM((cores, tiles, frames + 1, latent_ch, LANES), bf16),
        pltpu.VMEM((chan_count, depth_taps, latent_ch, out_ch), bf16),
        pltpu.VMEM((chan_count, 1, out_ch), f32),
        pltpu.VMEM((chan_count, 1, out_ch), f32),
        pltpu.VMEM((depth_taps, chans, out_ch), bf16),
        pltpu.VMEM((total_frames + 2, 9 * latent_ch, pixels), bf16),
        pltpu.VMEM((chan_count, total_frames, pixels, out_ch), f32),
        pltpu.VMEM((frames + 2, pixels + 2 * TSIDE, 3 * chans), bf16),
        pltpu.VMEM((frames, pixels, out_ch), f32),
        pltpu.VMEM((block_count, 2 * LANES, pixels), bf16),
        pltpu.VMEM((8, LANES), f32),
        pltpu.VMEM((8, LANES), f32),
        pltpu.VMEM((color_rows, pixels), f32),
        pltpu.VMEM((block_count, chan_count, color_rows, pixels), f32),
        dma((10,)),
        dma((tiles,)),
        dma((tiles,)),
        dma((tiles,)),
        dma((tiles,)),
    ]
    scratch += [dma((chan_count,)) for _ in range(8)]
    scratch += [dma, dma, dma((block_count, chan_count)), dma((block_count, chan_count))]
    colored = pl.pallas_call(
        functools.partial(kernel, sizes),
        out_shape=jax.ShapeDtypeStruct((colors, frames, own), f32),
        in_specs=[anywhere] * 10,
        out_specs=vmem,
        scratch_shapes=scratch,
        compiler_params=pltpu.CompilerParams(collective_id=0, has_side_effects=True),
    )(
        latents,
        tile_order,
        w_in,
        gain_in.reshape(1, -1),
        shift_in.reshape(1, -1),
        w_mid,
        gain_mid.reshape(1, -1),
        shift_mid.reshape(1, -1),
        w_out,
        blend_weight,
    )
    return jnp.transpose(colored, (1, 0, 2))


def solution(mesh):
    placed = (
        P("tm", "groups", "tile"),
        P("groups"),
        P(None, None, "chan"),
        P("chan"),
        P("chan"),
        P(None, None, "chan"),
        P("chan"),
        P("chan"),
        P(None, "chan"),
        P("groups", None),
    )
    sizes = (mesh.shape["tile"], mesh.shape["chan"], mesh.shape["tm"])
    return jax.shard_map(
        functools.partial(body, sizes),
        mesh=mesh,
        in_specs=placed,
        out_specs=P("tm", "groups", "tile"),
        check_vma=False,
    )
```

```python
import functools

import jax
import jax.numpy as jnp
from jax import lax
from jax.experimental import pallas as pl
from jax.experimental.pallas import tpu as pltpu
from jax.sharding import PartitionSpec as P

GROUPS = 32
TSIDE = 16
STRIDE = 12
GRID_X = 4
EPSILON = 1e-06
LANES = 128
MESH = pl.DeviceIdType.MESH


def place_matrix(down, across, kind):
    pixels = TSIDE * TSIDE
    pixel = lax.broadcasted_iota(jnp.int32, (2 * LANES, pixels), 0)
    slot = lax.broadcasted_iota(jnp.int32, (2 * LANES, pixels), 1)
    row = slot // TSIDE - STRIDE * down
    col = slot % TSIDE - STRIDE * across
    inside = (row >= 0) & (row < STRIDE) & (col >= 0) & (col < STRIDE)
    hit = inside & (pixel == row * STRIDE + col)
    return jnp.where(hit, 1.0, 0.0).astype(kind)


def group_sums(sums, squares, width):
    chans = sums.shape[1]
    chunks = chans // LANES
    rows = [v[:, LANES * i : LANES * (i + 1)] for v in (sums, squares) for i in range(chunks)]
    if len(rows) < 8:
        rows.append(jnp.zeros((8 - len(rows), LANES), jnp.float32))
    stacked = jnp.concatenate(rows, axis=0)
    left = lax.broadcasted_iota(jnp.int32, (LANES, LANES), 0) // width
    right = lax.broadcasted_iota(jnp.int32, (LANES, LANES), 1) // width
    same = jnp.where(left == right, 1.0, 0.0).astype(jnp.float32)
    return jnp.dot(
        stacked, same, precision=lax.Precision.HIGHEST, preferred_element_type=jnp.float32
    )


def half_affine(stats, chans, count, gain, shift):
    chunks = chans // LANES
    sums = jnp.concatenate([stats[i : i + 1] for i in range(chunks)], axis=1)
    squares = jnp.concatenate([stats[chunks + i : chunks + i + 1] for i in range(chunks)], axis=1)
    mean = sums / count
    variance = squares / count - mean * mean
    scale = lax.rsqrt(variance + EPSILON) * gain
    return 0.5 * scale, 0.5 * (shift - mean * scale)


def silu_of_half(half):
    return half + half * jnp.tanh(half)


def kernel(
    sizes,
    lat_hbm,
    order_hbm,
    w_in_ref,
    gain_in_ref,
    shift_in_ref,
    w_mid_ref,
    gain_mid_hbm,
    shift_mid_hbm,
    w_out_hbm,
    blend_hbm,
    out_ref,
    lat_ref,
    order_ref,
    gain_mid_ref,
    shift_mid_ref,
    w_out_ref,
    blend_ref,
    first_sums,
    lat,
    win,
    gains,
    shifts,
    mid,
    taps,
    first,
    hid,
    acc,
    place,
    stat_out,
    stat_in,
    col_out,
    col_in,
    local_sem,
    lat_s,
    lat_r,
    core_s,
    core_r,
    win_s,
    win_r,
    wcore_s,
    wcore_r,
    gain_s,
    gain_r,
    shift_s,
    shift_r,
    stat_s,
    stat_r,
    col_s,
    col_r,
):
    tiles, chan_count, cores = sizes
    frames, latent_ch, own = lat_hbm.shape
    extra = own - LANES
    total_frames = frames * cores
    depth_taps, _, out_ch = w_in_ref.shape
    chans = out_ch * chan_count
    width = chans // GROUPS
    pixels = TSIDE * TSIDE
    tile_rows = tiles // GRID_X
    tile = lax.axis_index("tile")
    chan = lax.axis_index("chan")
    tm = lax.axis_index("tm")
    other = cores - 1 - tm
    split = depth_taps // 2
    parts = ((0, split), (split, depth_taps - split))

    def remote(src, dst, send, recv, device):
        return pltpu.make_async_remote_copy(
            src_ref=src,
            dst_ref=dst,
            send_sem=send,
            recv_sem=recv,
            device_id=device,
            device_id_type=MESH,
        )

    barrier = pltpu.get_barrier_semaphore()
    for far in range(tiles):
        for side in range(chan_count):
            if far or side:
                pl.semaphore_signal(
                    barrier,
                    inc=1,
                    device_id={
                        "tile": lax.rem(tile + far, tiles),
                        "chan": lax.rem(chan + side, chan_count),
                    },
                    device_id_type=MESH,
                )
    pl.semaphore_signal(barrier, inc=1, device_id={"tm": other}, device_id_type=MESH)

    pairs = (
        (lat_hbm, lat_ref),
        (order_hbm, order_ref),
        (w_in_ref, win.at[chan]),
        (gain_in_ref, gains.at[chan]),
        (shift_in_ref, shifts.at[chan]),
        (gain_mid_hbm, gain_mid_ref),
        (shift_mid_hbm, shift_mid_ref),
        (w_out_hbm, w_out_ref),
        (blend_hbm, blend_ref),
        (w_mid_ref, mid),
    )
    loads = [
        pltpu.make_async_copy(src, dst, local_sem.at[i]) for i, (src, dst) in enumerate(pairs)
    ]
    for load in loads[:9]:
        load.start()

    blocks = [(down, across) for down in range(min(2, tile_rows)) for across in range(2)]
    for i, (down, across) in enumerate(blocks):
        place[i] = place_matrix(down, across, jnp.bfloat16)

    tail = jnp.zeros((latent_ch, LANES), jnp.float32)
    pixel = lax.broadcasted_iota(jnp.int32, (own, LANES), 0)
    lane = lax.broadcasted_iota(jnp.int32, (own, LANES), 1)
    loads[0].wait()
    for f in range(frames):
        lat[tm, tile, f] = lat_ref[f, :, 0:LANES]
        pick = (pixel >= LANES) & (lane == pixel - LANES + extra * f)
        tail = tail + jnp.dot(
            lat_ref[f],
            jnp.where(pick, 1.0, 0.0).astype(jnp.bfloat16),
            preferred_element_type=jnp.float32,
        )
    lat[tm, tile, frames] = tail.astype(jnp.bfloat16)
    taps[0:2] = jnp.zeros((2,) + taps.shape[1:], taps.dtype)
    edge = jnp.zeros((TSIDE, hid.shape[2]), hid.dtype)
    for s in range(frames + 2):
        hid[s, 0:TSIDE] = edge
        hid[s, TSIDE + pixels : 2 * TSIDE + pixels] = edge
    col_out[...] = jnp.zeros_like(col_out)

    pl.semaphore_wait(barrier, tiles * chan_count)

    mine = lat.at[tm, tile]
    sends = []
    for t, (start, size) in enumerate(parts):

        @pl.when(tm == t)
        def _():
            for d in range(1, chan_count):
                remote(
                    w_in_ref.at[pl.ds(start, size)],
                    win.at[chan, pl.ds(start, size)],
                    win_s.at[d],
                    win_r.at[d],
                    {"chan": lax.rem(chan + d, chan_count)},
                ).start()

    for step in range(1, tiles):
        d = jnp.where(2 * tile < tiles, tiles - step, step)
        copy = remote(
            mine, mine, lat_s.at[d], lat_r.at[d], {"tile": lax.rem(tile + d, tiles)}
        )
        copy.start()
        sends.append(copy)
    copy = remote(mine, mine, core_s.at[0], core_r.at[0], {"tm": other})
    copy.start()
    sends.append(copy)
    for d in range(1, chan_count):
        to = {"chan": lax.rem(chan + d, chan_count)}
        for src, dst, send, recv in (
            (gain_in_ref, gains, gain_s, gain_r),
            (shift_in_ref, shifts, shift_s, shift_r),
        ):
            copy = remote(src, dst.at[chan], send.at[d], recv.at[d], to)
            copy.start()
            sends.append(copy)

    loads[9].start()
    for d in range(1, tiles):
        slot = lat.at[tm, lax.rem(tile - d + tiles, tiles)]
        remote(slot, slot, lat_s.at[d], lat_r.at[d], {"tm": other}).wait_recv()
        copy = remote(slot, slot, core_s.at[d], core_r.at[d], {"tm": other})
        copy.start()
        sends.append(copy)
    for t, (start, size) in enumerate(parts):

        @pl.when(tm == t)
        def _():
            for d in range(1, chan_count):
                slot = win.at[lax.rem(chan - d + chan_count, chan_count), pl.ds(start, size)]
                remote(slot, slot, win_s.at[d], win_r.at[d], {"tm": other}).wait_recv()
                remote(slot, slot, wcore_s.at[d], wcore_r.at[d], {"tm": other}).start()

    for d in range(tiles):
        slot = lat.at[other, lax.rem(tile - d + tiles, tiles)]
        remote(slot, slot, core_s.at[d], core_r.at[d], {"tm": other}).wait_recv()

    loads[1].wait()
    window = jnp.zeros((total_frames * latent_ch, pixels), jnp.float32)
    for i, (down, across) in enumerate(blocks):
        block = tile + GRID_X * down + across
        held = jnp.int32(0)
        for d in range(tiles):
            held = jnp.where(order_ref[d] == block, d, held)
        valid = (lax.rem(tile, GRID_X) + across < GRID_X) & (tile // GRID_X + down < tile_rows)
        rows = []
        for t in range(cores):
            message = lat[t, held].astype(jnp.float32)
            for f in range(frames):
                rest = message[frames]
                if f:
                    rest = pltpu.roll(rest, LANES - extra * f, 1)
                rows.append(jnp.concatenate([message[f], rest], axis=1))
        image = jnp.where(valid, jnp.concatenate(rows, axis=0), 0.0).astype(jnp.bfloat16)
        window = window + jnp.dot(image, place[i], preferred_element_type=jnp.float32)
    slot_id = lax.broadcasted_iota(jnp.int32, window.shape, 1)
    row, col = slot_id // TSIDE, slot_id % TSIDE
    for down in range(3):
        for across in range(3):
            offset = (down - 1) * TSIDE + across - 1
            moved = window if offset == 0 else pltpu.roll(window, -offset % pixels, 1)
            inside = (
                (row + down >= 1)
                & (row + down <= TSIDE)
                & (col + across >= 1)
                & (col + across <= TSIDE)
            )
            moved = jnp.where(inside, moved, 0.0).astype(jnp.bfloat16)
            at = (3 * down + across) * latent_ch
            taps[2 : 2 + total_frames, at : at + latent_ch, :] = moved.reshape(
                total_frames, latent_ch, pixels
            )

    loads[2].wait()
    zero = jnp.zeros((8, out_ch), jnp.float32)
    for d in range(chan_count):
        source = lax.rem(chan - d + chan_count, chan_count)
        if d:
            for t, (start, size) in enumerate(parts):

                @pl.when(tm != t)
                def _():
                    slot = win.at[source, pl.ds(start, size)]
                    remote(slot, slot, wcore_s.at[d], wcore_r.at[d], {"tm": other}).wait_recv()

        def first_step(g, carry):
            sums, squares = carry
            for f in (2 * g, 2 * g + 1):
                value = lax.dot_general(
                    taps[pl.ds(f, 3)].reshape(depth_taps * latent_ch, pixels),
                    win[source].reshape(depth_taps * latent_ch, out_ch),
                    (((0,), (0,)), ((), ())),
                    preferred_element_type=jnp.float32,
                )
                first[source, f] = value
                folded = value.reshape(pixels // 8, 8, out_ch)
                sums = sums + jnp.sum(folded, axis=0)
                squares = squares + jnp.sum(folded * folded, axis=0)
            return sums, squares

        sums, squares = lax.fori_loop(0, total_frames // 2, first_step, (zero, zero))
        first_sums[source, 0:1] = jnp.sum(sums, axis=0, keepdims=True)
        first_sums[source, 1:2] = jnp.sum(squares, axis=0, keepdims=True)
    for load in loads[3:9]:
        load.wait()
    for d in range(1, chan_count):
        slot_chan = lax.rem(chan - d + chan_count, chan_count)
        for dst, send, recv in ((gains, gain_s, gain_r), (shifts, shift_s, shift_r)):
            slot = dst.at[slot_chan]
            remote(slot, slot, send.at[d], recv.at[d], {"tm": other}).wait_recv()
    count = total_frames * width * pixels
    stats = group_sums(
        jnp.concatenate([first_sums[c, 0:1] for c in range(chan_count)], axis=1),
        jnp.concatenate([first_sums[c, 1:2] for c in range(chan_count)], axis=1),
        width,
    )
    scale, offset = half_affine(
        stats,
        chans,
        count,
        jnp.concatenate([gains[c] for c in range(chan_count)], axis=1),
        jnp.concatenate([shifts[c] for c in range(chan_count)], axis=1),
    )

    step_rows = 2 * TSIDE
    steps = pixels // step_rows
    col = lax.broadcasted_iota(jnp.int32, (step_rows, out_ch), 0) % TSIDE

    def hidden_rows(s, r):
        frame = frames * tm - 2 + s
        known = frame >= 0
        frame = jnp.maximum(frame, 0)
        for c in range(chan_count):
            channels = slice(out_ch * c, out_ch * (c + 1))
            value = silu_of_half(
                first[c, frame, step_rows * r : step_rows * (r + 1), :] * scale[:, channels]
                + offset[:, channels]
            )
            value = jnp.where(known, value, 0.0)
            before = jnp.where(col == 0, 0.0, pltpu.roll(value, 1, 0))
            after = jnp.where(col == TSIDE - 1, 0.0, pltpu.roll(value, step_rows - 1, 0))
            for e, piece in enumerate((before, value, after)):
                hid[
                    s,
                    TSIDE + step_rows * r : TSIDE + step_rows * (r + 1),
                    chans * e + out_ch * c : chans * e + out_ch * (c + 1),
                ] = piece.astype(jnp.bfloat16)

    def hidden_step(s, carry):
        for r in range(steps):
            hidden_rows(s, r)
        return carry

    batch = 2 if frames % 2 == 0 else 1
    lax.fori_loop(0, batch + 2, hidden_step, 0)
    loads[9].wait()

    sums = squares = jnp.zeros((8, out_ch), jnp.float32)
    for at in range(0, frames, batch):
        ahead = [
            (s, r)
            for s in range(at + batch + 2, min(at + 2 * batch, frames) + 2)
            for r in range(steps)
        ]
        share = -(-len(ahead) // 9)
        total = None
        for a in range(3):
            for b in range(3):
                value = jnp.dot(
                    hid[at + a : at + a + batch, TSIDE * b : TSIDE * b + pixels, :].reshape(
                        batch * pixels, 3 * chans
                    ),
                    mid[9 * a + 3 * b : 9 * a + 3 * b + 3].reshape(3 * chans, out_ch),
                    preferred_element_type=jnp.float32,
                )
                total = value if total is None else total + value
                for s, r in ahead[share * (3 * a + b) : share * (3 * a + b + 1)]:
                    hidden_rows(s, r)
        acc[at : at + batch] = total.reshape(batch, pixels, out_ch)
        folded = total.reshape(batch * pixels // 8, 8, out_ch)
        sums = sums + jnp.sum(folded, axis=0)
        squares = squares + jnp.sum(folded * folded, axis=0)
    stats = group_sums(
        jnp.sum(sums, axis=0, keepdims=True), jnp.sum(squares, axis=0, keepdims=True), width
    )
    stat_out[...] = stats
    stat_copy = remote(stat_out, stat_in, stat_s, stat_r, {"tm": other})
    stat_copy.start()
    stat_copy.wait()
    stats = stats + stat_in[...]
    scale, offset = half_affine(stats, out_ch, count, gain_mid_ref[...], shift_mid_ref[...])
    colors = out_ref.shape[0]
    for f in range(frames):
        upper = silu_of_half(acc[f] * scale + offset).astype(jnp.bfloat16)
        color = lax.dot_general(
            w_out_ref[...], upper, (((1,), (1,)), ((), ())), preferred_element_type=jnp.float32
        )
        for o in range(colors):
            col_out[frames * o + f : frames * o + f + 1, :] = color[o : o + 1]

    def tile_valid_to(down, across):
        return (lax.rem(tile, GRID_X) + across < GRID_X) & (tile // GRID_X + down < tile_rows)

    def tile_valid_from(down, across):
        return (lax.rem(tile, GRID_X) >= across) & (tile // GRID_X >= down)

    def color_copy(i, d, hop):
        return remote(
            col_out,
            col_in.at[i, d],
            col_s.at[i, d],
            col_r.at[i, d],
            {
                "tile": lax.rem(tile + hop, tiles),
                "chan": lax.rem(chan + d, chan_count),
            },
        )

    for i, (down, across) in reversed(list(enumerate(blocks))):
        for d in reversed(range(chan_count)):
            if i or d:
                pl.when(tile_valid_to(down, across))(
                    color_copy(i, d, GRID_X * down + across).start
                )

    rows = col_out.shape[0]
    row_id = lax.broadcasted_iota(jnp.int32, (rows, pixels), 0)
    blended = jnp.zeros((rows, 2 * LANES), jnp.float32)
    for i, (down, across) in enumerate(blocks):
        hop = GRID_X * down + across
        here = tile_valid_from(down, across)
        for d in range(chan_count):
            if i or d:
                pl.when(here)(color_copy(i, d, hop).wait_recv)
        color = col_out[...] if i == 0 else col_in[i, 0]
        for d in range(1, chan_count):
            color = color + col_in[i, d]
        weight = blend_ref[pl.ds(lax.rem(tile - hop + tiles, tiles), 1), :]
        color = jnp.where(row_id == colors * frames, 1.0, color) * weight
        color = jnp.where(here, color, 0.0)
        blended = blended + lax.dot_general(
            color,
            place[i].astype(jnp.float32),
            (((1,), (1,)), ((), ())),
            precision=lax.Precision.HIGHEST,
            preferred_element_type=jnp.float32,
        )
    result = blended / blended[colors * frames : colors * frames + 1]
    for o in range(colors):
        out_ref[o] = result[frames * o : frames * (o + 1), :own]

    for copy in sends:
        copy.wait_send()
    for t, (start, size) in enumerate(parts):

        @pl.when(tm == t)
        def _():
            for d in range(1, chan_count):
                slot = win.at[lax.rem(chan - d + chan_count, chan_count), pl.ds(start, size)]
                remote(slot, slot, win_s.at[d], win_r.at[d], {"tm": other}).wait_send()
                remote(slot, slot, wcore_s.at[d], wcore_r.at[d], {"tm": other}).wait_send()

    for i, (down, across) in enumerate(blocks):
        for d in range(chan_count):
            if i or d:
                pl.when(tile_valid_to(down, across))(
                    color_copy(i, d, GRID_X * down + across).wait_send
                )


def body(
    sizes,
    latents,
    tile_order,
    w_in,
    gain_in,
    shift_in,
    w_mid,
    gain_mid,
    shift_mid,
    w_out,
    blend_weight,
):
    tiles, chan_count, cores = sizes
    frames, latent_ch, own = latents.shape
    depth_taps, chans, out_ch = w_mid.shape
    total_frames = frames * cores
    pixels = TSIDE * TSIDE
    colors = w_out.shape[0]
    vmem = pl.BlockSpec(memory_space=pltpu.VMEM)
    anywhere = pl.BlockSpec(memory_space=pl.ANY)
    bf16, f32 = jnp.bfloat16, jnp.float32
    block_count = 2 * min(2, tiles // GRID_X)
    color_rows = -(-(colors * frames + 1) // 8) * 8
    dma = pltpu.SemaphoreType.DMA
    smem = pltpu.SMEM
    scratch = [
        pltpu.VMEM(latents.shape, bf16),
        smem(tile_order.shape, jnp.int32),
        pltpu.VMEM((1, out_ch), f32),
        pltpu.VMEM((1, out_ch), f32),
        pltpu.VMEM(w_out.shape, bf16),
        pltpu.VMEM(blend_weight.shape, f32),
        pltpu.VMEM((chan_count, 8, out_ch), f32),
        pltpu.VMEM((cores, tiles, frames + 1, latent_ch, LANES), bf16),
        pltpu.VMEM((chan_count, depth_taps, latent_ch, out_ch), bf16),
        pltpu.VMEM((chan_count, 1, out_ch), f32),
        pltpu.VMEM((chan_count, 1, out_ch), f32),
        pltpu.VMEM((depth_taps, chans, out_ch), bf16),
        pltpu.VMEM((total_frames + 2, 9 * latent_ch, pixels), bf16),
        pltpu.VMEM((chan_count, total_frames, pixels, out_ch), f32),
        pltpu.VMEM((frames + 2, pixels + 2 * TSIDE, 3 * chans), bf16),
        pltpu.VMEM((frames, pixels, out_ch), f32),
        pltpu.VMEM((block_count, 2 * LANES, pixels), bf16),
        pltpu.VMEM((8, LANES), f32),
        pltpu.VMEM((8, LANES), f32),
        pltpu.VMEM((color_rows, pixels), f32),
        pltpu.VMEM((block_count, chan_count, color_rows, pixels), f32),
        dma((10,)),
        dma((tiles,)),
        dma((tiles,)),
        dma((tiles,)),
        dma((tiles,)),
    ]
    scratch += [dma((chan_count,)) for _ in range(8)]
    scratch += [dma, dma, dma((block_count, chan_count)), dma((block_count, chan_count))]
    colored = pl.pallas_call(
        functools.partial(kernel, sizes),
        out_shape=jax.ShapeDtypeStruct((colors, frames, own), f32),
        in_specs=[anywhere] * 10,
        out_specs=vmem,
        scratch_shapes=scratch,
        compiler_params=pltpu.CompilerParams(collective_id=0, has_side_effects=True),
    )(
        latents,
        tile_order,
        w_in,
        gain_in.reshape(1, -1),
        shift_in.reshape(1, -1),
        w_mid,
        gain_mid.reshape(1, -1),
        shift_mid.reshape(1, -1),
        w_out,
        blend_weight,
    )
    return jnp.transpose(colored, (1, 0, 2))


def solution(mesh):
    placed = (
        P("tm", "groups", "tile"),
        P("groups"),
        P(None, None, "chan"),
        P("chan"),
        P("chan"),
        P(None, None, "chan"),
        P("chan"),
        P("chan"),
        P(None, "chan"),
        P("groups", None),
    )
    sizes = (mesh.shape["tile"], mesh.shape["chan"], mesh.shape["tm"])
    return jax.shard_map(
        functools.partial(body, sizes),
        mesh=mesh,
        in_specs=placed,
        out_specs=P("tm", "groups", "tile"),
        check_vma=False,
    )
```
